32 devices in a mesh: replica: 2 (over y), fsdp: 16 (over z, x, core).
Axes of the slice: x: 2, y: 2, z: 4, core: 2. Of those that a mesh axis runs over, the one named last changes fastest.
Arguments:
- tokens: float32 [6144, 768], P(('replica', 'fsdp')), may hold values from -6 to 6
- segment: int32 [32, 192], P(('replica', 'fsdp')), may hold values from 0 to 7, never falling along the last dimension, each value on 1 to 96 neighbouring positions
- cotangent: float32 [6144, 768], P(('replica', 'fsdp')), may hold values from -6 to 6
- norm1_gain: bfloat16 [768], P('fsdp'), may hold values from 0.5 to 1.5
- norm1_shift: bfloat16 [768], P('fsdp'), may hold values from -1 to 1
- qkv_weight: bfloat16 [768, 2304], P('fsdp'), may hold values from -2 to 2
- qv_bias: bfloat16 [1536], P('fsdp'), may hold values from -1 to 1
- out_weight: bfloat16 [768, 768], P('fsdp'), may hold values from -0.625 to 0.625
- out_bias: bfloat16 [768], P('fsdp'), may hold values from -1 to 1
- norm2_gain: bfloat16 [768], P('fsdp'), may hold values from 0.5 to 1.5
- norm2_shift: bfloat16 [768], P('fsdp'), may hold values from -1 to 1
- fc1_weight: bfloat16 [768, 3072], P('fsdp'), may hold values from -0.109375 to 0.109375
- fc1_bias: bfloat16 [3072], P('fsdp'), may hold values from -1.4 to 1.4
- fc2_weight: bfloat16 [3072, 768], P('fsdp'), may hold values from -0.15625 to 0.15625
- fc2_bias: bfloat16 [768], P('fsdp'), may hold values from -1 to 1
Outputs:
- layer_out: float32 [6144, 768], P(('replica', 'fsdp'))
- grad_tokens: float32 [6144, 768], P(('replica', 'fsdp'))
- grad_norm1_gain: float32 [768], P('fsdp')
- grad_norm1_shift: float32 [768], P('fsdp')
- grad_qkv_weight: float32 [768, 2304], P('fsdp')
- grad_qv_bias: float32 [1536], P('fsdp')
- grad_out_weight: float32 [768, 768], P('fsdp')
- grad_out_bias: float32 [768], P('fsdp')
- grad_norm2_gain: float32 [768], P('fsdp')
- grad_norm2_shift: float32 [768], P('fsdp')
- grad_fc1_weight: float32 [768, 3072], P('fsdp')
- grad_fc1_bias: float32 [3072], P('fsdp')
- grad_fc2_weight: float32 [3072, 768], P('fsdp')
- grad_fc2_bias: float32 [768], P('fsdp')
The draws below stay inside these ranges and needn't reach their ends.
Inputs may be any that keep to these rules, and one draw needn't show every extreme that they name: `segment`: along each sequence the numbers never fall; a run of equal numbers is one document.
All inputs are finite; a program needn't handle non-finite values.
Results may differ from the reference program's by a relative error of at most 0.025.
The reference program's roundings to bfloat16 on the way count: a program that leaves them out, or rounds other values in their place, can miss the bound.
Values may be sent and summed in bfloat16 or wider, within the bound.
No kernel may reach another device: no remote copies, remote signals or barrier semaphores. Data moves between devices by JAX's collectives and lax.ppermute only.
A program may use at most 128 MiB of HBM per device.

```python
import math
import jax
import jax.numpy as jnp
import numpy as np
from jax import lax

D = 768
HEADS = 12
HEAD_DIM = 64
FF = 3072
L = 192
SEQS = 32
TOKENS = 6144


def draw_qkv_weight(key, part):
    base = jax.random.normal(key, (D, 3 * D), jnp.float32) * D ** (-0.5)
    return jnp.clip(base, -2.0, 2.0).astype(jnp.bfloat16)


def draw_fc1_bias(key, part):
    sign_key = jax.random.fold_in(key, 11)
    size_key = jax.random.fold_in(key, 12)
    signs = jnp.where(jax.random.bernoulli(sign_key, 0.5, (FF,)), 1.0, -1.0)
    sizes = 0.6 + 0.8 * jax.random.beta(size_key, 2.0, 2.0, (FF,))
    return (signs * sizes).astype(jnp.bfloat16)


def block_levels(own_key, shape, cuts, low, high):
    loudness = 1.0
    for position, parts in cuts:
        steps = jax.random.uniform(jax.random.fold_in(jax.random.fold_in(own_key, 6), position), (parts,), jnp.float32, low / len(cuts), high / len(cuts))
        loudness = loudness * jnp.repeat(jnp.exp(steps), shape[position] // parts).reshape((-1,) + (1,) * (len(shape) - 1 - position))
    return loudness


def length_profile(number_of, total, limit, slope):
    portions = [(1 << 20) // math.isqrt(standing ** slope) + 1 for standing in range(2, number_of + 1)]
    spare, holding = total - limit - (number_of - 1), [1] * (number_of - 1)
    while spare > 0:
        candidates = [i for i in range(number_of - 1) if holding[i] < limit]
        whole, left = sum([portions[i] for i in candidates]), spare
        for i in candidates:
            addition = min(limit - holding[i], max(1, left * portions[i] // whole), spare)
            holding[i] = holding[i] + addition
            spare = spare - addition
    return np.array([limit] + holding)


def ragged(key, count, total, reach, slope):
    if count == 2:
        one = jax.random.randint(key, (), max(1, total - reach), min(reach, total - 1) + 1)
        return jnp.stack([one, total - one])
    sizes = jnp.asarray(length_profile(count, total, reach, slope), jnp.int32)
    couples = (count - 1) // 2
    donor, sink = sizes[1:1 + 2 * couples:2], sizes[2:2 + 2 * couples:2]
    margin = jnp.minimum(donor - 1, reach - sink)
    shifted = jax.random.randint(jax.random.fold_in(key, 1), (couples,), 0, 1 << 20) % (margin + 1)
    sizes = sizes.at[1:1 + 2 * couples:2].set(donor - shifted).at[2:2 + 2 * couples:2].set(sink + shifted)
    return sizes[jax.random.permutation(jax.random.fold_in(key, 2), count)]


def centred(own_key, extent, width, reach, pieces=(), held_as=jnp.bfloat16):
    result = width * jax.random.normal(own_key, extent, jnp.float32)
    if pieces:
        result = result * block_levels(own_key, extent, pieces, -0.22, 0.18)
    return jnp.clip(result, -reach, reach).astype(held_as)


def setup_inputs(seed: int = 0) -> dict:
    splits = jax.random.split(jax.random.key(seed), 16)
    return {
        "tokens": centred(splits[0], (TOKENS, D), 1.0, 6.0, ((0, 32),), jnp.float32),
        "segment": jax.vmap(lambda own: jnp.searchsorted(jnp.cumsum(ragged(own, 8, L, L // 2, 0)), jnp.arange(L), side="right"))(jax.random.split(splits[1], SEQS)).reshape((SEQS, L)).astype(jnp.int32),
        "cotangent": centred(splits[2], (TOKENS, D), 1.0, 6.0, ((0, 32),), jnp.float32),
        "norm1_gain": jnp.clip(1.0 + 0.1 * jax.random.normal(splits[3], (D,), jnp.float32), 0.5, 1.5).astype(jnp.bfloat16),
        "norm1_shift": centred(splits[4], (D,), 0.2, 1.0, ((0, 16),)),
        "qkv_weight": draw_qkv_weight(jax.random.fold_in(splits[15], 71), 0),
        "qv_bias": centred(splits[6], (2 * D,), 0.2, 1.0, ((0, 16),)),
        "out_weight": centred(splits[7], (D, D), (D // 8) ** -0.5, 0.625, ((0, 16),)),
        "out_bias": centred(splits[8], (D,), 0.2, 1.0, ((0, 16),)),
        "norm2_gain": jnp.clip(1.0 + 0.1 * jax.random.normal(splits[9], (D,), jnp.float32), 0.5, 1.5).astype(jnp.bfloat16),
        "norm2_shift": centred(splits[10], (D,), 0.2, 1.0, ((0, 16),)),
        "fc1_weight": centred(splits[11], (D, FF), (4 * D) ** -0.5, 0.109375, ((0, 16),)),
        "fc1_bias": draw_fc1_bias(jax.random.fold_in(splits[15], 71), 0),
        "fc2_weight": centred(splits[13], (FF, D), (FF // 2) ** -0.5, 0.15625, ((0, 16),)),
        "fc2_bias": centred(splits[14], (D,), 0.2, 1.0, ((0, 16),)),
    }


EPSILON = 1e-05

def layer_norm(inputs, gain_vec, shift_vec):
    average = lax.optimization_barrier(jnp.mean(inputs, axis=-1, keepdims=True))
    centered = inputs - average
    variance = lax.optimization_barrier(jnp.mean(centered * centered, axis=-1, keepdims=True))
    inv_std = lax.rsqrt(variance + EPSILON)
    normed = centered * inv_std
    return (normed * gain_vec.astype(jnp.float32) + shift_vec.astype(jnp.float32), normed, inv_std)

def norm_back(grad_out, normed, inv_std, gain_vec):
    grad_norm = grad_out * gain_vec.astype(jnp.float32)
    first = lax.optimization_barrier(jnp.mean(grad_norm, axis=-1, keepdims=True))
    second = lax.optimization_barrier(jnp.mean(grad_norm * normed, axis=-1, keepdims=True))
    grad_in = inv_std * (grad_norm - first - normed * second)
    return (grad_in, lax.optimization_barrier(jnp.sum(grad_out * normed, axis=0)), lax.optimization_barrier(jnp.sum(grad_out, axis=0)))

def allowed_pairs(segment):
    length = segment.shape[1]
    causal = jnp.arange(length)[:, None] >= jnp.arange(length)[None, :]
    same_doc = segment[:, :, None] == segment[:, None, :]
    return (same_doc & causal[None])[:, None]

def masked_scores(queries, key_rows, allowed):
    scores = jnp.einsum('bqhe,bkhe->bhqk', queries.astype(jnp.float32), key_rows.astype(jnp.float32)) * HEAD_DIM ** (-0.5)
    return jnp.where(allowed, scores, -1e+30)

def one_block(tok_blk, seg_blk, cot_blk, params):
    gain_one, shift_one, qkv_weight, qv_bias, out_weight, out_bias, gain_two, shift_two, fc1_weight, fc1_bias, fc2_weight, fc2_bias = params
    seq_count = seg_blk.shape[0]
    row_count = tok_blk.shape[0]
    f32 = jnp.float32
    bf16 = jnp.bfloat16
    normed1, hat_one, rstd_one = layer_norm(tok_blk, gain_one, shift_one)
    n_one = normed1.astype(bf16)
    proj = jnp.dot(n_one, qkv_weight, preferred_element_type=f32)
    qv_f = qv_bias.astype(f32)
    queries = (proj[:, :D] + qv_f[:D]).astype(bf16).reshape(seq_count, L, HEADS, HEAD_DIM)
    key_rows = proj[:, D:2 * D].astype(bf16).reshape(seq_count, L, HEADS, HEAD_DIM)
    values = (proj[:, 2 * D:] + qv_f[D:]).astype(bf16).reshape(seq_count, L, HEADS, HEAD_DIM)
    allowed = allowed_pairs(seg_blk)
    scores = masked_scores(queries, key_rows, allowed)
    top = lax.optimization_barrier(jnp.max(scores, axis=-1, keepdims=True))
    log_total = top + jnp.log(lax.optimization_barrier(jnp.sum(jnp.exp(scores - top), axis=-1, keepdims=True)))
    probs = jnp.where(allowed, jnp.exp(scores - log_total), 0.0)
    probs_b = probs.astype(bf16)
    attn = jnp.einsum('bhqk,bkhe->bqhe', probs_b.astype(f32), values.astype(f32))
    attn = attn.reshape(row_count, D).astype(bf16)
    resid = tok_blk + jnp.dot(attn, out_weight, preferred_element_type=f32) + out_bias.astype(f32)
    normed2, hat_two, rstd_two = layer_norm(resid, gain_two, shift_two)
    n_two = normed2.astype(bf16)
    pre = jnp.dot(n_two, fc1_weight, preferred_element_type=f32) + fc1_bias.astype(f32)
    act = jnp.maximum(pre, 0.0).astype(bf16)
    layer_out = resid + jnp.dot(act, fc2_weight, preferred_element_type=f32) + fc2_bias.astype(f32)
    cot_b = cot_blk.astype(bf16)
    g_fc2_w = jnp.dot(act.T, cot_b, preferred_element_type=f32)
    g_fc2_b = lax.optimization_barrier(jnp.sum(cot_blk, axis=0))
    d_act = jnp.dot(cot_b, fc2_weight.T, preferred_element_type=f32)
    d_pre = jnp.where(pre > 0, d_act, 0.0)
    g_fc1_b = lax.optimization_barrier(jnp.sum(d_pre, axis=0))
    d_pre_b = d_pre.astype(bf16)
    g_fc1_w = jnp.dot(n_two.T, d_pre_b, preferred_element_type=f32)
    d_normed2 = jnp.dot(d_pre_b, fc1_weight.T, preferred_element_type=f32)
    d_two, g_gain_two, g_shift_two = norm_back(d_normed2, hat_two, rstd_two, gain_two)
    d_resid = cot_blk + d_two
    d_resid_b = d_resid.astype(bf16)
    g_out_w = jnp.dot(attn.T, d_resid_b, preferred_element_type=f32)
    g_out_b = lax.optimization_barrier(jnp.sum(d_resid, axis=0))
    d_attn = jnp.dot(d_resid_b, out_weight.T, preferred_element_type=f32).astype(bf16)
    d_attn = d_attn.reshape(seq_count, L, HEADS, HEAD_DIM)
    d_values = jnp.einsum('bhqk,bqhe->bkhe', probs_b.astype(f32), d_attn.astype(f32))
    d_probs = jnp.einsum('bqhe,bkhe->bhqk', d_attn.astype(f32), values.astype(f32))
    delta = lax.optimization_barrier(jnp.sum(probs * d_probs, axis=-1, keepdims=True))
    d_scores = (probs * (d_probs - delta) * HEAD_DIM ** (-0.5)).astype(bf16)
    d_queries = jnp.einsum('bhqk,bkhe->bqhe', d_scores.astype(f32), key_rows.astype(f32)).reshape(row_count, D)
    d_keys = jnp.einsum('bhqk,bqhe->bkhe', d_scores.astype(f32), queries.astype(f32)).reshape(row_count, D)
    d_values = d_values.reshape(row_count, D)
    g_qv_b = jnp.concatenate([lax.optimization_barrier(jnp.sum(d_queries, axis=0)), lax.optimization_barrier(jnp.sum(d_values, axis=0))])
    d_proj = jnp.concatenate([d_queries, d_keys, d_values], axis=1).astype(bf16)
    g_qkv_w = jnp.dot(n_one.T, d_proj, preferred_element_type=f32)
    d_normed1 = jnp.dot(d_proj, qkv_weight.T, preferred_element_type=f32)
    d_one, g_gain_one, g_shift_one = norm_back(d_normed1, hat_one, rstd_one, gain_one)
    grad_in = d_resid + d_one
    grads = (g_gain_one, g_shift_one, g_qkv_w, g_qv_b, g_out_w, g_out_b, g_gain_two, g_shift_two, g_fc1_w, g_fc1_b, g_fc2_w, g_fc2_b)
    return (layer_out, grad_in, grads)

def reference(tokens, segment, cotangent, norm1_gain, norm1_shift, qkv_weight, qv_bias, out_weight, out_bias, norm2_gain, norm2_shift, fc1_weight, fc1_bias, fc2_weight, fc2_bias):
    params = (norm1_gain, norm1_shift, qkv_weight, qv_bias, out_weight, out_bias, norm2_gain, norm2_shift, fc1_weight, fc1_bias, fc2_weight, fc2_bias)
    block_seqs = math.gcd(SEQS, 16)
    block_count = SEQS // block_seqs
    tok_all = tokens.reshape(block_count, block_seqs * L, D)
    cot_all = cotangent.reshape(block_count, block_seqs * L, D)
    seg_all = segment.reshape(block_count, block_seqs, L)
    zeros = tuple((jnp.zeros(p.shape, jnp.float32) for p in params))

    def step_fn(carry, inputs):
        tok_blk, seg_blk, cot_blk = inputs
        layer_out, grad_in, grads = one_block(tok_blk, seg_blk, cot_blk, params)
        carry = tuple((a + b for a, b in zip(carry, grads)))
        return (carry, (layer_out, grad_in))
    totals, (outs_all, grads_all) = lax.scan(step_fn, zeros, (tok_all, seg_all, cot_all))
    factor = TOKENS ** (-0.5)
    scaled = tuple((t * factor for t in totals))
    return (outs_all.reshape(TOKENS, D), grads_all.reshape(TOKENS, D)) + scaled
```

```python
import functools

import jax
import jax.numpy as jnp
from jax import lax
from jax.experimental import pallas as pl
from jax.experimental.pallas import tpu as pltpu
from jax.sharding import PartitionSpec as P


D = 768
HEADS = 12
HEAD_DIM = 64
FF = 3072
L = 192
PAIRS = HEADS // 2
UNITS = 4

EPSILON = 1e-05
F32 = jnp.float32
BF16 = jnp.bfloat16
NT = (((1,), (1,)), ((), ()))
TN = (((0,), (0,)), ((), ()))
ANY = pl.BlockSpec(memory_space=pl.ANY)
VMEM = pl.BlockSpec(memory_space=pltpu.VMEM)
SMEM = pl.BlockSpec(memory_space=pltpu.SMEM)


def mm(a, b, dims=None):
    if dims is None:
        return jnp.dot(a, b, preferred_element_type=F32)
    return lax.dot_general(a, b, dims, preferred_element_type=F32)


def normalize(v):
    centered = v - jnp.mean(v, axis=-1, keepdims=True)
    inv_std = lax.rsqrt(jnp.mean(centered * centered, axis=-1, keepdims=True) + EPSILON)
    return centered * inv_std, inv_std


def norm_back(grad_out, normed, inv_std, gain):
    grad_norm = grad_out * gain
    first = jnp.mean(grad_norm, axis=-1, keepdims=True)
    second = jnp.mean(grad_norm * normed, axis=-1, keepdims=True)
    grad_in = inv_std * (grad_norm - first - normed * second)
    return (
        grad_in,
        jnp.sum(grad_out * normed, axis=0, keepdims=True),
        jnp.sum(grad_out, axis=0, keepdims=True),
    )


def start_assembly(at, depth, group, parts, w_ref, sem, by_rows):
    z, x, y, c = at[0], at[1], at[2], at[3]

    def place(src, d, other_x, core, unit, count):
        zz = lax.rem(z - d + depth, depth)
        xx = 1 - x if other_x else x
        shard = zz * 4 + xx * 2 + core
        span = pl.ds(unit, count)
        dst = w_ref.at[shard, span] if by_rows else w_ref.at[span, shard]
        pltpu.make_async_copy(src, dst, sem).start()

    half = len(parts) // 2
    for side, core in ((parts[:half], c), (parts[half:], 1 - c)):
        own, near, cross, zs, xs, ys, ps, qs = side
        place(own.at[group], 0, False, core, 0, UNITS)
        place(near.at[group], 0, True, core, 2 * y, 2)
        place(cross.at[group], 0, True, core, 2 * (1 - y), 2)
        for d in range(1, depth):
            place(zs.at[d - 1], d, False, core, 2 * y, 2)
            place(xs.at[d - 1], d, True, core, 2 * y, 2)
            place(ys.at[d - 1], d, False, core, 2 * (1 - y), 2)
            place(ps.at[pl.ds(d - 1, 1)], d, True, core, 2 * (1 - y), 1)
            place(qs.at[pl.ds(d - 1, 1)], d, True, core, 2 * (1 - y) + 1, 1)


def wait_assembly(w_ref, sem):
    pltpu.make_async_copy(w_ref, w_ref, sem).wait()


def split_cores(value, c, t_ref, mine_ref, theirs_ref):
    t_ref[...] = value.T.reshape(t_ref.shape)
    for j in range(t_ref.shape[0] // 2):
        mine_ref[j] = t_ref[2 * j + c]
        theirs_ref[j] = t_ref[2 * j + 1 - c]


def head_mask(width):
    return lax.broadcasted_iota(jnp.int32, (1, width), 1) < HEAD_DIM


def pair_cols(p):
    return slice(2 * HEAD_DIM * p, 2 * HEAD_DIM * (p + 1))


def softmax_rows(q2, k2, first, low, allowed):
    keep = low if first else jnp.logical_not(low)
    qm = jnp.where(keep, q2, jnp.zeros_like(q2))
    scores = jnp.where(allowed, mm(qm, k2, NT) * HEAD_DIM ** (-0.5), -1e30)
    top = jnp.max(scores, axis=-1, keepdims=True)
    raised = jnp.exp(scores - top)
    return raised * (1.0 / jnp.sum(raised, axis=-1, keepdims=True))


def allowed_pairs(seg_col, seg_row):
    rows = lax.broadcasted_iota(jnp.int32, (L, L), 0)
    cols = lax.broadcasted_iota(jnp.int32, (L, L), 1)
    return (seg_col == seg_row) & (rows >= cols)


def attend_kernel(depth, group, at, tok, seg_col, seg_row, vecs, *refs):
    parts, refs = refs[:16], refs[16:]
    q_ref, k_ref, v_ref, resid_ref, n2_ref, mine_ref, theirs_ref, w_out = refs[:8]
    w_ref, t_ref, attn_ref, sem, out_sem = refs[8:]
    c = at[3]
    start_assembly(at, depth, group, parts, w_ref, sem, False)
    normed, _ = normalize(tok[...])
    n1 = (normed * vecs[0:1] + vecs[1:2]).astype(BF16)
    split_cores(n1, c, t_ref, mine_ref.at[0], theirs_ref.at[0])
    allowed = allowed_pairs(seg_col[...], seg_row[...])
    low = head_mask(2 * HEAD_DIM)
    wait_assembly(w_ref, sem)
    keep_w = pltpu.make_async_copy(w_ref, w_out, out_sem)
    keep_w.start()
    q_ref[...] = (mm(n1, w_ref[0].reshape(D, D)) + vecs[6:7]).astype(BF16)
    k_ref[...] = mm(n1, w_ref[1].reshape(D, D)).astype(BF16)
    v_ref[...] = (mm(n1, w_ref[2].reshape(D, D)) + vecs[7:8]).astype(BF16)
    for p in range(PAIRS):
        cols = pair_cols(p)
        q2, k2, v2 = q_ref[:, cols], k_ref[:, cols], v_ref[:, cols]
        outs = [
            mm(softmax_rows(q2, k2, first, low, allowed).astype(BF16), v2)
            for first in (True, False)
        ]
        attn_ref[:, cols] = jnp.where(low, outs[0], outs[1]).astype(BF16)
    attn = attn_ref[...]
    split_cores(attn, c, t_ref, mine_ref.at[1], theirs_ref.at[1])
    resid = tok[...] + mm(attn, w_ref[3].reshape(D, D)) + vecs[2:3]
    resid_ref[...] = resid
    normed, _ = normalize(resid)
    n2 = (normed * vecs[3:4] + vecs[4:5]).astype(BF16)
    n2_ref[...] = n2
    split_cores(n2, c, t_ref, mine_ref.at[2], theirs_ref.at[2])
    keep_w.wait()


def up_kernel(depth, group, at, n2, bias, *refs):
    parts, refs = refs[:16], refs[16:]
    act_ref, mine_ref, theirs_ref, w_out, w_ref, t_ref, sem, out_sem = refs
    start_assembly(at, depth, group, parts, w_ref, sem, False)
    wait_assembly(w_ref, sem)
    keep_w = pltpu.make_async_copy(w_ref, w_out, out_sem)
    keep_w.start()
    for u in range(UNITS):
        cols = slice(u * D, (u + 1) * D)
        pre = mm(n2[...], w_ref[u].reshape(D, D)) + bias[:, cols]
        act_ref[:, cols] = jnp.maximum(pre, 0.0).astype(BF16)
    split_cores(act_ref[...], at[3], t_ref, mine_ref, theirs_ref)
    keep_w.wait()


def down_back_kernel(depth, group, at, act, cot_b, *refs):
    parts, refs = refs[:16], refs[16:]
    d_pre_ref, g_bias, w_out, w_ref, sem, out_sem = refs
    start_assembly(at, depth, group, parts, w_ref, sem, True)
    wait_assembly(w_ref, sem)
    keep_w = pltpu.make_async_copy(w_ref, w_out, out_sem)
    keep_w.start()
    d_act = mm(cot_b[...], w_ref[...].reshape(FF, D), NT)
    d_pre = jnp.where(act[...] > 0, d_act, 0.0)
    g_bias[...] = jnp.sum(d_pre, axis=0, keepdims=True)
    d_pre_ref[...] = d_pre.astype(BF16)
    keep_w.wait()


def down_kernel(act, resid, vecs, w, out):
    out[...] = resid[...] + mm(act[...], w[...].reshape(FF, D)) + vecs[5:6]


def up_back_kernel(d_pre, resid, cot, vecs, w_up, w_att, d_resid_ref, d_resid_b_ref, d_attn_ref, g_ref):
    d_norm = jnp.zeros((L, D), F32)
    for u in range(UNITS):
        d_norm = d_norm + mm(d_pre[:, u * D : (u + 1) * D], w_up[u].reshape(D, D), NT)
    normed, inv_std = normalize(resid[...])
    d_two, g_gain, g_shift = norm_back(d_norm, normed, inv_std, vecs[3:4])
    d_resid = cot[...] + d_two
    d_resid_b = d_resid.astype(BF16)
    d_resid_ref[...] = d_resid
    d_resid_b_ref[...] = d_resid_b
    g_ref[...] = jnp.concatenate(
        [
            g_gain,
            g_shift,
            jnp.sum(d_resid, axis=0, keepdims=True),
            jnp.sum(cot[...], axis=0, keepdims=True),
        ],
        axis=0,
    )
    d_attn_ref[...] = mm(d_resid_b, w_att[3].reshape(D, D), NT).astype(BF16)


def attend_back_kernel(q_ref, k_ref, v_ref, d_attn, seg_col, seg_row, d_proj_ref, g_ref):
    allowed = allowed_pairs(seg_col[...], seg_row[...])
    low = head_mask(2 * HEAD_DIM)
    for p in range(PAIRS):
        cols = pair_cols(p)
        q2, k2, v2, do2 = q_ref[:, cols], k_ref[:, cols], v_ref[:, cols], d_attn[:, cols]
        got = []
        for first in (True, False):
            keep = low if first else jnp.logical_not(low)
            probs = softmax_rows(q2, k2, first, low, allowed)
            d_probs = mm(jnp.where(keep, do2, jnp.zeros_like(do2)), v2, NT)
            delta = jnp.sum(probs * d_probs, axis=-1, keepdims=True)
            d_scores = (probs * (d_probs - delta) * HEAD_DIM ** (-0.5)).astype(BF16)
            got.append(
                (mm(d_scores, k2), mm(d_scores, q2, TN), mm(probs.astype(BF16), do2, TN))
            )
        dq, dk, dv = (jnp.where(low, a, b) for a, b in zip(*got))
        for i, part in enumerate((dq, dk, dv)):
            d_proj_ref[:, i * D + cols.start : i * D + cols.stop] = part.astype(BF16)
        g_ref[:, cols] = jnp.concatenate(
            [jnp.sum(dq, axis=0, keepdims=True), jnp.sum(dv, axis=0, keepdims=True)], axis=0
        )


def qkv_back_kernel(d_proj, tok, d_resid, vecs, w_att, grad_ref, g_ref):
    d_norm = jnp.zeros((L, D), F32)
    for u in range(3):
        d_norm = d_norm + mm(d_proj[:, u * D : (u + 1) * D], w_att[u].reshape(D, D), NT)
    normed, inv_std = normalize(tok[...])
    d_one, g_gain, g_shift = norm_back(d_norm, normed, inv_std, vecs[0:1])
    grad_ref[...] = d_resid[...] + d_one
    g_ref[...] = jnp.concatenate([g_gain, g_shift], axis=0)


def deal_units(at, depth, dw_ref, outs):
    z, x, y = at[0], at[1], at[2]
    send_x, send_y, keep_x, keep_y = outs
    for d in range(depth):
        zz = lax.rem(z + d, depth)
        for other in (0, 1):
            h = 1 - y if other else y
            xx = 1 - x if other else x
            send_x[d, other] = dw_ref[zz * 2 + 1 - x, 2 * h]
            keep_x[d, other] = dw_ref[zz * 2 + x, 2 * h]
            send_y[d, other] = dw_ref[zz * 2 + xx, 2 * (1 - y) + 1]
            keep_y[d, other] = dw_ref[zz * 2 + xx, 2 * y + 1]


def down_grad_kernel(depth, at, mine, theirs, cot, cot_p, *refs):
    outs, dw_ref = refs[:4], refs[4]
    rows = mine.shape[0] * mine.shape[1]
    dw = mm(mine[...].reshape(rows, L), cot[...]) + mm(theirs[...].reshape(rows, L), cot_p[...])
    dw_ref[...] = dw.astype(BF16).reshape(dw_ref.shape)
    deal_units(at, depth, dw_ref, outs)


def wide_grad_kernel(depth, ways, at, *refs):
    n = len(ways)
    ins, outs, dw_ref = refs[: 4 * n], refs[4 * n : 4 * n + 4], refs[-1]
    unit = 0
    for i, units in enumerate(ways):
        mine, theirs, right, right_p = ins[4 * i : 4 * i + 4]
        rows = mine.shape[0] * mine.shape[1]
        for j in range(units):
            cols = slice(j * D, (j + 1) * D)
            dw = mm(mine[...].reshape(rows, L), right[:, cols])
            dw = dw + mm(theirs[...].reshape(rows, L), right_p[:, cols])
            dw_ref[:, unit] = dw.astype(BF16).reshape(mine.shape[0], -1, D)
            unit += 1
    deal_units(at, depth, dw_ref, outs)


def call(kernel, name, outs, in_specs, out_specs, scratch, *args):
    return pl.pallas_call(
        kernel,
        name=name,
        out_shape=outs,
        in_specs=in_specs,
        out_specs=out_specs,
        scratch_shapes=scratch,
        compiler_params=pltpu.CompilerParams(vmem_limit_bytes=56 * 1024 * 1024),
    )(*args)


def shape(dims, dtype=BF16):
    return jax.ShapeDtypeStruct(dims, dtype)


class Links:
    def __init__(self, owners):
        self.depth = owners // 4
        spots = [(z, x, c) for z in range(self.depth) for x in range(2) for c in range(2)]
        self.core_perm = [(self.flat(z, x, c), self.flat(z, x, 1 - c)) for z, x, c in spots]
        self.x_perm = [(self.flat(z, x, c), self.flat(z, 1 - x, c)) for z, x, c in spots]
        self.z_perms = [
            [(self.flat(z, x, c), self.flat((z + d) % self.depth, x, c)) for z, x, c in spots]
            for d in range(self.depth)
        ]

    @staticmethod
    def flat(z, x, c):
        return z * 4 + x * 2 + c

    def core(self, v):
        return lax.ppermute(v, "fsdp", self.core_perm)

    def x(self, v):
        return lax.ppermute(v, "fsdp", self.x_perm)

    def y(self, v):
        return lax.ppermute(v, "replica", [(0, 1), (1, 0)])

    def z(self, v, d):
        return lax.ppermute(v, "fsdp", self.z_perms[d])

    def total(self, v):
        v = v + self.core(v)
        v = v + self.x(v)
        v = v + self.y(v)
        return self.around(v)

    def around(self, v):
        got = [self.z(v, d) for d in range(1, self.depth)]
        for g in got:
            v = v + g
        return v


def after(value, *others):
    return lax.optimization_barrier((value,) + others)[0]


def on_device_linked(
    owners,
    tokens,
    segment,
    cotangent,
    norm1_gain,
    norm1_shift,
    qkv_weight,
    qv_bias,
    out_weight,
    out_bias,
    norm2_gain,
    norm2_shift,
    fc1_weight,
    fc1_bias,
    fc2_weight,
    fc2_bias,
):
    link = Links(owners)
    depth = link.depth
    f = lax.axis_index("fsdp")
    y = lax.axis_index("replica")
    z, x, c = f // 4, (f // 2) % 2, f % 2
    at = jnp.stack([z, x, y, c]).astype(jnp.int32)
    rows = D // owners
    factor = (tokens.shape[0] * 2 * owners) ** (-0.5)

    small = (
        norm1_gain,
        norm1_shift,
        out_bias,
        norm2_gain,
        norm2_shift,
        fc2_bias,
        qv_bias,
        fc1_bias,
    )
    widths = [s.shape[0] for s in small]
    row = jnp.concatenate(small)[None]
    mine = lax.broadcasted_iota(jnp.int32, (owners, 1), 0) == f
    table = jnp.where(mine, row, jnp.zeros_like(row))
    table = table + link.core(table)
    table = table + link.x(table)
    table = link.around(table).astype(F32)
    full, start = [], 0
    for w in widths:
        full.append(table[:, start : start + w].reshape(1, owners * w))
        start += w
    qv = full[6].reshape(2, D)
    vecs = jnp.concatenate(full[:6] + [qv], axis=0)
    up_bias = full[7]

    own = jnp.stack(
        [
            jnp.stack([qkv_weight[:, :D], qkv_weight[:, D : 2 * D], qkv_weight[:, 2 * D :], out_weight]),
            fc1_weight.reshape(rows, UNITS, D).transpose(1, 0, 2),
            fc2_weight.reshape(UNITS, rows, D),
        ]
    )
    halves = lax.dynamic_slice_in_dim(own, 2 * y, 2, 1)
    near = link.x(halves)
    own_c = link.core(own)
    near_c = link.core(near)
    cross = link.y(near)
    cross_c = link.core(cross)
    parts, gate = [], None
    for g in range(3):
        half = halves[g]
        if gate is not None:
            half = after(half, *gate)
        zl = [link.z(half, d) for d in range(1, depth)]
        gate = zl
        zs = jnp.stack(zl)
        xs, ys = link.x(zs), link.y(zs)
        zs_c = link.core(zs)
        ps, qs = link.y(xs[:, 0]), link.x(ys[:, 1])
        xs_c, ys_c = link.core(xs), link.core(ys)
        ps_c, qs_c = link.core(ps), link.core(qs)
        parts.append(
            (own, near, cross, zs, xs, ys, ps, qs, own_c, near_c, cross_c, zs_c, xs_c, ys_c, ps_c, qs_c)
        )

    cot_b = cotangent.astype(BF16)
    cot_p = link.core(cot_b)
    seg_col, seg_row = segment.reshape(L, 1), segment.reshape(1, L)
    n_half = owners // 2
    wide = (UNITS, owners, rows, D)
    tall = (owners, UNITS, rows, D)
    sems = [pltpu.SemaphoreType.DMA(()), pltpu.SemaphoreType.DMA(())]

    q, k, v, resid, n2, mine3, theirs3, w_att = call(
        functools.partial(attend_kernel, depth, 0),
        "attend",
        [shape((L, D))] * 3
        + [shape((L, D), F32), shape((L, D))]
        + [shape((3, n_half, rows, L))] * 2
        + [shape(wide)],
        [SMEM] + [VMEM] * 4 + [ANY] * 16,
        [VMEM] * 7 + [ANY],
        [pltpu.VMEM(wide, BF16), pltpu.VMEM((owners, rows, L), BF16), pltpu.VMEM((L, D), BF16)] + sems,
        at,
        tokens,
        seg_col,
        seg_row,
        vecs,
        *parts[0],
    )
    got3 = link.core(theirs3)

    ff_rows = FF // owners
    act, act_mine, act_theirs, w_up = call(
        functools.partial(up_kernel, depth, 1),
        "up",
        [shape((L, FF))] + [shape((n_half, ff_rows, L))] * 2 + [shape(wide)],
        [SMEM] + [VMEM] * 2 + [ANY] * 16,
        [VMEM] * 3 + [ANY],
        [pltpu.VMEM(wide, BF16), pltpu.VMEM((owners, ff_rows, L), BF16)] + sems,
        at,
        n2,
        up_bias,
        *parts[1],
    )
    act_got = link.core(act_theirs)

    dealt = [shape((depth, 2, rows, D))] * 4
    dw_scratch = [pltpu.VMEM((n_half, UNITS, rows, D), BF16)]

    down_units = call(
        functools.partial(down_grad_kernel, depth),
        "down_grad",
        dealt,
        [SMEM] + [VMEM] * 4,
        [VMEM] * 4,
        dw_scratch,
        at,
        act_mine,
        act_got,
        cot_b,
        cot_p,
    )

    d_pre, g_up_bias, w_down = call(
        functools.partial(down_back_kernel, depth, 2),
        "down_back",
        [shape((L, FF)), shape((1, FF), F32), shape(tall)],
        [SMEM] + [VMEM] * 2 + [ANY] * 16,
        [VMEM] * 2 + [ANY],
        [pltpu.VMEM(tall, BF16)] + sems,
        at,
        act,
        cot_b,
        *parts[2],
    )
    d_pre_p = link.core(d_pre)

    d_resid, d_resid_b, d_attn, g_mid = call(
        up_back_kernel,
        "up_back",
        [shape((L, D), F32), shape((L, D)), shape((L, D)), shape((4, D), F32)],
        [VMEM] * 6,
        [VMEM] * 4,
        [],
        d_pre,
        resid,
        cotangent,
        vecs,
        w_up,
        w_att,
    )
    d_resid_p = link.core(d_resid_b)

    up_units = call(
        functools.partial(wide_grad_kernel, depth, (UNITS,)),
        "up_grad",
        dealt,
        [SMEM] + [VMEM] * 4,
        [VMEM] * 4,
        dw_scratch,
        at,
        mine3[2],
        got3[2],
        d_pre,
        d_pre_p,
    )

    d_proj, g_qv = call(
        attend_back_kernel,
        "attend_back",
        [shape((L, 3 * D)), shape((2, D), F32)],
        [VMEM] * 6,
        [VMEM] * 2,
        [],
        q,
        k,
        v,
        d_attn,
        seg_col,
        seg_row,
    )
    d_proj_p = link.core(d_proj)

    layer_out = call(
        down_kernel,
        "down",
        shape((L, D), F32),
        [VMEM] * 4,
        VMEM,
        [],
        act,
        resid,
        vecs,
        w_down,
    )

    att_units = call(
        functools.partial(wide_grad_kernel, depth, (3, 1)),
        "att_grad",
        dealt,
        [SMEM] + [VMEM] * 8,
        [VMEM] * 4,
        dw_scratch,
        at,
        mine3[0],
        got3[0],
        d_proj,
        d_proj_p,
        mine3[1],
        got3[1],
        d_resid_b,
        d_resid_p,
    )

    grad_tokens, g_one = call(
        qkv_back_kernel,
        "qkv_back",
        [shape((L, D), F32), shape((2, D), F32)],
        [VMEM] * 5,
        [VMEM] * 2,
        [],
        d_proj,
        tokens,
        d_resid,
        vecs,
        w_att,
    )

    def reduce_units(units):
        send_x, send_y, keep_x, keep_y = units
        first = keep_x + link.x(send_x)
        second = keep_y + link.y(send_y)
        p = first[:, 0] + link.y(first[:, 1])
        q = second[:, 0] + link.x(second[:, 1])
        both = jnp.stack([p, q], axis=1)
        total = both[0].astype(F32)
        for d in range(1, depth):
            total = total + link.z(both[d], d).astype(F32)
        total = (total * factor).astype(BF16)
        other = link.y(total)
        low = jnp.where(y == 0, total, other)
        high = jnp.where(y == 0, other, total)
        return low.astype(F32), high.astype(F32)

    down_low, down_high = reduce_units(down_units)
    up_low, up_high = reduce_units(up_units)
    att_low, att_high = reduce_units(att_units)
    g_down = jnp.concatenate([down_low, down_high]).reshape(UNITS * rows, D)
    g_up = jnp.concatenate([up_low[0], up_low[1], up_high[0], up_high[1]], axis=1)
    g_qkv = jnp.concatenate([att_low[0], att_low[1], att_high[0]], axis=1)
    g_out = att_high[1]

    early = link.total(jnp.concatenate([g_up_bias, g_mid.reshape(1, 4 * D)], axis=1)) * factor
    late = link.total(jnp.concatenate([g_qv.reshape(1, 2 * D), g_one.reshape(1, 2 * D)], axis=1)) * factor

    def cut(source, offset, whole):
        part = whole // owners
        return lax.dynamic_slice(source, (0, offset + f * part), (1, part))[0]

    return (
        layer_out,
        grad_tokens,
        cut(late, 2 * D, D),
        cut(late, 3 * D, D),
        g_qkv,
        cut(late, 0, 2 * D),
        g_out,
        cut(early, FF + 2 * D, D),
        cut(early, FF, D),
        cut(early, FF + D, D),
        g_up,
        cut(early, 0, FF),
        g_down,
        cut(early, FF + 3 * D, D),
    )


def layer_norm(inputs, gain_vec, shift_vec):
    average = jnp.mean(inputs, axis=-1, keepdims=True)
    centered = inputs - average
    variance = jnp.mean(centered * centered, axis=-1, keepdims=True)
    inv_std = lax.rsqrt(variance + EPSILON)
    normed = centered * inv_std
    return (normed * gain_vec.astype(jnp.float32) + shift_vec.astype(jnp.float32), normed, inv_std)


def plain_norm_back(grad_out, normed, inv_std, gain_vec):
    grad_norm = grad_out * gain_vec.astype(jnp.float32)
    first = jnp.mean(grad_norm, axis=-1, keepdims=True)
    second = jnp.mean(grad_norm * normed, axis=-1, keepdims=True)
    grad_in = inv_std * (grad_norm - first - normed * second)
    return (grad_in, jnp.sum(grad_out * normed, axis=0), jnp.sum(grad_out, axis=0))


def plain_allowed(segment):
    length = segment.shape[1]
    causal = jnp.arange(length)[:, None] >= jnp.arange(length)[None, :]
    same_doc = segment[:, :, None] == segment[:, None, :]
    return (same_doc & causal[None])[:, None]


def masked_scores(queries, key_rows, allowed):
    scores = jnp.einsum(
        "bqhe,bkhe->bhqk", queries, key_rows, preferred_element_type=jnp.float32
    ) * HEAD_DIM ** (-0.5)
    return jnp.where(allowed, scores, -1e30)


def on_device_plain(
    tokens,
    segment,
    cotangent,
    norm1_gain,
    norm1_shift,
    qkv_weight,
    qv_bias,
    out_weight,
    out_bias,
    norm2_gain,
    norm2_shift,
    fc1_weight,
    fc1_bias,
    fc2_weight,
    fc2_bias,
):
    f32 = jnp.float32
    bf16 = jnp.bfloat16
    seq_count = segment.shape[0]
    row_count = tokens.shape[0]
    gathered = (
        lax.all_gather(norm1_gain, "fsdp", axis=0, tiled=True),
        lax.all_gather(norm1_shift, "fsdp", axis=0, tiled=True),
        lax.all_gather(qkv_weight, "fsdp", axis=0, tiled=True),
        lax.all_gather(qv_bias, "fsdp", axis=0, tiled=True),
        lax.all_gather(out_weight, "fsdp", axis=0, tiled=True),
        lax.all_gather(out_bias, "fsdp", axis=0, tiled=True),
        lax.all_gather(norm2_gain, "fsdp", axis=0, tiled=True),
        lax.all_gather(norm2_shift, "fsdp", axis=0, tiled=True),
        lax.all_gather(fc1_weight, "fsdp", axis=0, tiled=True),
        lax.all_gather(fc1_bias, "fsdp", axis=0, tiled=True),
        lax.all_gather(fc2_weight, "fsdp", axis=0, tiled=True),
        lax.all_gather(fc2_bias, "fsdp", axis=0, tiled=True),
    )
    (
        gain_one,
        shift_one,
        qkv_full,
        qv_full,
        out_full,
        out_bias_full,
        gain_two,
        shift_two,
        up_full,
        up_bias_full,
        down_full,
        down_bias_full,
    ) = gathered
    normed1, hat_one, rstd_one = layer_norm(tokens, gain_one, shift_one)
    n_one = normed1.astype(bf16)
    proj = jnp.dot(n_one, qkv_full, preferred_element_type=f32)
    qv_f = qv_full.astype(f32)
    queries = (proj[:, :D] + qv_f[:D]).astype(bf16).reshape(seq_count, L, HEADS, HEAD_DIM)
    key_rows = proj[:, D : 2 * D].astype(bf16).reshape(seq_count, L, HEADS, HEAD_DIM)
    values = (proj[:, 2 * D :] + qv_f[D:]).astype(bf16).reshape(seq_count, L, HEADS, HEAD_DIM)
    allowed = plain_allowed(segment)
    scores = masked_scores(queries, key_rows, allowed)
    top = jnp.max(scores, axis=-1, keepdims=True)
    log_total = top + jnp.log(jnp.sum(jnp.exp(scores - top), axis=-1, keepdims=True))
    probs_b = jnp.where(allowed, jnp.exp(scores - log_total), 0.0).astype(bf16)
    attn = jnp.einsum("bhqk,bkhe->bqhe", probs_b, values, preferred_element_type=f32)
    attn = attn.reshape(row_count, D).astype(bf16)
    resid = tokens + jnp.dot(attn, out_full, preferred_element_type=f32) + out_bias_full.astype(f32)
    normed2, hat_two, rstd_two = layer_norm(resid, gain_two, shift_two)
    n_two = normed2.astype(bf16)
    pre = jnp.dot(n_two, up_full, preferred_element_type=f32) + up_bias_full.astype(f32)
    act = jnp.maximum(pre, 0.0).astype(bf16)
    layer_out = (
        resid + jnp.dot(act, down_full, preferred_element_type=f32) + down_bias_full.astype(f32)
    )
    again = (
        lax.all_gather(norm1_gain, "fsdp", axis=0, tiled=True),
        lax.all_gather(norm1_shift, "fsdp", axis=0, tiled=True),
        lax.all_gather(qkv_weight, "fsdp", axis=0, tiled=True),
        lax.all_gather(qv_bias, "fsdp", axis=0, tiled=True),
        lax.all_gather(out_weight, "fsdp", axis=0, tiled=True),
        lax.all_gather(out_bias, "fsdp", axis=0, tiled=True),
        lax.all_gather(norm2_gain, "fsdp", axis=0, tiled=True),
        lax.all_gather(norm2_shift, "fsdp", axis=0, tiled=True),
        lax.all_gather(fc1_weight, "fsdp", axis=0, tiled=True),
        lax.all_gather(fc1_bias, "fsdp", axis=0, tiled=True),
        lax.all_gather(fc2_weight, "fsdp", axis=0, tiled=True),
        lax.all_gather(fc2_bias, "fsdp", axis=0, tiled=True),
    )
    (
        gain_one,
        shift_one,
        qkv_full,
        qv_full,
        out_full,
        out_bias_full,
        gain_two,
        shift_two,
        up_full,
        up_bias_full,
        down_full,
        down_bias_full,
    ) = again
    cot_b = cotangent.astype(bf16)
    g_fc2_b = jnp.sum(cotangent, axis=0)
    d_act = jnp.dot(cot_b, down_full.T, preferred_element_type=f32)
    d_pre = jnp.where(pre > 0, d_act, 0.0)
    g_fc1_b = jnp.sum(d_pre, axis=0)
    d_pre_b = d_pre.astype(bf16)
    d_normed2 = jnp.dot(d_pre_b, up_full.T, preferred_element_type=f32)
    d_two, g_gain_two, g_shift_two = plain_norm_back(d_normed2, hat_two, rstd_two, gain_two)
    d_resid = cotangent + d_two
    d_resid_b = d_resid.astype(bf16)
    g_out_b = jnp.sum(d_resid, axis=0)
    d_attn = jnp.dot(d_resid_b, out_full.T, preferred_element_type=f32).astype(bf16)
    d_attn = d_attn.reshape(seq_count, L, HEADS, HEAD_DIM)
    scores = masked_scores(queries, key_rows, allowed)
    probs = jnp.where(allowed, jnp.exp(scores - log_total), 0.0)
    probs_b = probs.astype(bf16)
    d_values = jnp.einsum("bhqk,bqhe->bkhe", probs_b, d_attn, preferred_element_type=f32)
    d_probs = jnp.einsum("bqhe,bkhe->bhqk", d_attn, values, preferred_element_type=f32)
    delta = jnp.sum(probs * d_probs, axis=-1, keepdims=True)
    d_scores = (probs * (d_probs - delta) * HEAD_DIM ** (-0.5)).astype(bf16)
    d_queries = jnp.einsum(
        "bhqk,bkhe->bqhe", d_scores, key_rows, preferred_element_type=f32
    ).reshape(row_count, D)
    d_keys = jnp.einsum("bhqk,bqhe->bkhe", d_scores, queries, preferred_element_type=f32).reshape(
        row_count, D
    )
    d_values = d_values.reshape(row_count, D)
    g_qv_b = jnp.concatenate([jnp.sum(d_queries, axis=0), jnp.sum(d_values, axis=0)])
    d_proj = jnp.concatenate([d_queries, d_keys, d_values], axis=1).astype(bf16)
    d_normed1 = jnp.dot(d_proj, qkv_full.T, preferred_element_type=f32)
    d_one, g_gain_one, g_shift_one = plain_norm_back(d_normed1, hat_one, rstd_one, gain_one)
    grad_tokens = d_resid + d_one
    replicas = lax.axis_size("replica")
    owners = lax.axis_size("fsdp")
    factor = (row_count * replicas * owners) ** (-0.5)
    operand_pairs = ((n_one, d_proj), (attn, d_resid_b), (n_two, d_pre_b), (act, cot_b))
    mats = tuple(
        (
            jnp.dot(left.T, right, preferred_element_type=f32) * factor
            for left, right in operand_pairs
        )
    )
    owned = (
        lax.psum_scatter(g_gain_one * factor, "fsdp", scatter_dimension=0, tiled=True),
        lax.psum_scatter(g_shift_one * factor, "fsdp", scatter_dimension=0, tiled=True),
        lax.psum_scatter(mats[0], "fsdp", scatter_dimension=0, tiled=True),
        lax.psum_scatter(g_qv_b * factor, "fsdp", scatter_dimension=0, tiled=True),
        lax.psum_scatter(mats[1], "fsdp", scatter_dimension=0, tiled=True),
        lax.psum_scatter(g_out_b * factor, "fsdp", scatter_dimension=0, tiled=True),
        lax.psum_scatter(g_gain_two * factor, "fsdp", scatter_dimension=0, tiled=True),
        lax.psum_scatter(g_shift_two * factor, "fsdp", scatter_dimension=0, tiled=True),
        lax.psum_scatter(mats[2], "fsdp", scatter_dimension=0, tiled=True),
        lax.psum_scatter(g_fc1_b * factor, "fsdp", scatter_dimension=0, tiled=True),
        lax.psum_scatter(mats[3], "fsdp", scatter_dimension=0, tiled=True),
        lax.psum_scatter(g_fc2_b * factor, "fsdp", scatter_dimension=0, tiled=True),
    )
    summed = lax.psum(
        (
            owned[0],
            owned[1],
            owned[2],
            owned[3],
            owned[4],
            owned[5],
            owned[6],
            owned[7],
            owned[8],
            owned[9],
            owned[10],
            owned[11],
        ),
        "replica",
    )
    return (layer_out, grad_tokens) + tuple(summed)


def solution(mesh):
    in_specs = (
        P(("replica", "fsdp"), None),
        P(("replica", "fsdp"), None),
        P(("replica", "fsdp"), None),
        P("fsdp"),
        P("fsdp"),
        P("fsdp", None),
        P("fsdp"),
        P("fsdp", None),
        P("fsdp"),
        P("fsdp"),
        P("fsdp"),
        P("fsdp", None),
        P("fsdp"),
        P("fsdp", None),
        P("fsdp"),
    )
    out_specs = (
        P(("replica", "fsdp"), None),
        P(("replica", "fsdp"), None),
        P("fsdp"),
        P("fsdp"),
        P("fsdp", None),
        P("fsdp"),
        P("fsdp", None),
        P("fsdp"),
        P("fsdp"),
        P("fsdp"),
        P("fsdp", None),
        P("fsdp"),
        P("fsdp", None),
        P("fsdp"),
    )
    replicas, owners = mesh.shape["replica"], mesh.shape["fsdp"]
    on_device = on_device_plain
    if replicas == 2 and owners % 4 == 0 and (D // owners) % 16 == 0:
        on_device = functools.partial(on_device_linked, owners)
    return jax.shard_map(
        on_device, mesh=mesh, in_specs=in_specs, out_specs=out_specs, check_vma=False
    )
```
